256 devices in a mesh: occ: 16 (over z_hi, y, core), vir: 16 (over z_lo, x).
Axes of the slice: x: 4, y: 4, z: 8 (z_hi: 2, z_lo: 4; z = z_hi * 4 + z_lo), core: 2. Of those that a mesh axis runs over, the one named last changes fastest.
Arguments:
- amplitudes: bfloat16 [8192, 8192], P('occ', 'vir'), may hold values from -6 to 6
- hole_integrals: bfloat16 [8192, 8192], P('occ'), may hold values from -0.1875 to 0.1875
- particle_integrals: bfloat16 [8192, 8192], P('vir'), may hold values from -0.25 to 0.25
- occ_irrep: int32 [128], replicated, may hold values from 0 to 7
- vir_irrep: int32 [128], replicated, may hold values from 0 to 7
- occ_energy: float32 [8192], P('occ'), may hold values from -1.5 to -0.5
- vir_energy: float32 [8192], P('vir'), may hold values from 0.5 to 2.5
Outputs:
- update: float32 [8192, 8192], P('vir', 'occ')
The draws below stay inside these ranges and needn't reach their ends.
All inputs are finite; a program needn't handle non-finite values.
Results may differ from the reference program's by a relative error of at most 0.0003.
Values may be sent and summed in bfloat16 or wider, within the bound.
No kernel may reach another device: no remote copies, remote signals or barrier semaphores. Data moves between devices by JAX's collectives and lax.ppermute only.
A program may use at most 128 MiB of HBM per device.

```python
import jax
import jax.numpy as jnp

TILE = 64
P_SIZE = 8192
Q = 8192


def with_ends(array, own_key, low, top_value):
    spot = [jax.random.randint(jax.random.fold_in(own_key, axis), (), 0, length) for axis, length in enumerate(array.shape)]
    widest = array.shape.index(max(array.shape))
    neighbour = spot[:widest] + [(spot[widest] + 1) % array.shape[widest]] + spot[widest + 1:]
    return array.at[tuple(spot)].set(low).at[tuple(neighbour)].set(top_value)


def with_spikes(entries, key, source, target, blocks, factor):
    owner, partner = [(jnp.arange(entries.shape[position]) // (entries.shape[position] // blocks)).reshape([-1 if axis == position else 1 for axis in range(entries.ndim)]) for position in (source, target)]
    chosen = jax.random.permutation(key, blocks)[partner]
    strong = (owner == chosen) | (owner == (partner + blocks // 2) % blocks)
    return jnp.where(strong, factor * entries, entries)


def steps_of(stream_key, extent, shards, low, top_value):
    gain = 1.0
    for dim, blocks in shards:
        steps = jax.random.uniform(jax.random.fold_in(jax.random.fold_in(stream_key, 6), dim), (blocks,), jnp.float32, low / len(shards), top_value / len(shards))
        gain = gain * jnp.repeat(jnp.exp(steps), extent[dim] // blocks).reshape((-1,) + (1,) * (len(extent) - 1 - dim))
    return gain


def gaussian(stream_key, dims, width, limit, split=(), dtype=jnp.bfloat16):
    result = jax.random.normal(stream_key, dims, jnp.float32) * width
    if len(split) > 0:
        result = steps_of(stream_key, dims, split, -0.22, 0.18) * result
    return jnp.clip(result, min=-limit, max=limit).astype(dtype)


def heavy_noise(stream_key, shape, spread, most, pieces, heavy, dtype=jnp.bfloat16):
    result = spread * jax.random.normal(stream_key, shape, jnp.float32)
    if pieces:
        result = result * steps_of(stream_key, shape, pieces, -0.22, 0.18)
    return jnp.clip(with_spikes(result, jax.random.fold_in(stream_key, 3), *heavy), -most, most).astype(dtype)


def setup_inputs(seed: int = 0) -> dict:
    keys = jax.random.split(jax.random.key(seed), 8)
    amplitudes = gaussian(keys[0], (P_SIZE, Q), 1.0, 6.0, ((0, 16), (1, 16)))
    hole_integrals = gaussian(keys[1], (P_SIZE, P_SIZE), (P_SIZE // 8) ** -0.5, 0.1875, ((0, 16),))
    particle_integrals = heavy_noise(keys[2], (Q, Q), (Q // 8) ** -0.5, 0.25, ((0, 16),), (0, 1, 16, 2.0))
    occ_irrep = with_ends(jax.random.randint(keys[3], (P_SIZE // TILE,), 0, 8), jax.random.fold_in(keys[3], 1), 0, 7).astype(jnp.int32)
    vir_irrep = with_ends(jax.random.randint(keys[4], (Q // TILE,), 0, 8), jax.random.fold_in(keys[4], 1), 0, 7).astype(jnp.int32)
    occ_energy = jnp.clip(-1.5 + 1.0 * jax.random.uniform(keys[5], (P_SIZE,), jnp.float32) ** steps_of(keys[5], (P_SIZE,), ((0, 16),), -0.2, 0.2), -1.5, -0.5)
    vir_energy = jnp.clip(0.5 + 2.0 * jax.random.uniform(keys[6], (Q,), jnp.float32) ** steps_of(keys[6], (Q,), ((0, 16),), -0.2, 0.2), 0.5, 2.5)
    return {"amplitudes": amplitudes, "hole_integrals": hole_integrals, "particle_integrals": particle_integrals, "occ_irrep": occ_irrep, "vir_irrep": vir_irrep, "occ_energy": occ_energy, "vir_energy": vir_energy}


def reference(amplitudes, hole_integrals, particle_integrals, occ_irrep, vir_irrep, occ_energy, vir_energy):
    occ_labels = jnp.repeat(occ_irrep, TILE)
    vir_labels = jnp.repeat(vir_irrep, TILE)
    zero_value = jnp.zeros((), jnp.bfloat16)
    hole_masked = jnp.where(occ_labels[:, None] == occ_labels[None, :], hole_integrals, zero_value)
    particle_masked = jnp.where(vir_labels[:, None] == vir_labels[None, :], particle_integrals, zero_value)
    hole = jnp.dot(hole_masked, amplitudes, preferred_element_type=jnp.float32)
    particle = jnp.dot(amplitudes, particle_masked, preferred_element_type=jnp.float32)
    energy_gap = vir_energy[:, None] - occ_energy[None, :]
    return (hole + particle).T / energy_gap
```

```python
import functools

import jax
import jax.numpy as jnp
from jax import lax
from jax.experimental import pallas as pl
from jax.experimental.pallas import tpu as pltpu
from jax.sharding import Mesh, PartitionSpec as P

TILE = 64
F32, BF16 = jnp.float32, jnp.bfloat16
AXES = ("zh", "y", "c", "zl", "x")
OCC, VIR = ("zh", "y", "c"), ("zl", "x")
NY, NC, NX, NZ = 4, 2, 4, 4
LIMIT = 48 * 1024 * 1024


def ring(n, d):
    return [(i, (i + d) % n) for i in range(n)]


def shift(a, axis, n, d):
    return lax.ppermute(a, axis, ring(n, d))


def params(n):
    return pltpu.CompilerParams(dimension_semantics=("arbitrary",) * n, vmem_limit_bytes=LIMIT)


def cost(blocks, n):
    return pl.CostEstimate(
        flops=2 * blocks * n**3, bytes_accessed=blocks * 2 * n * n * 2 + 4 * n * n, transcendentals=0
    )


def hole_kernel(idx, occ, klab0, klab1, w0, w1, t0, t1, *rest, has_acc):
    if has_acc:
        acc, out, masked = rest
    else:
        out, masked = rest
    j = pl.program_id(0)

    @pl.when(j == 0)
    def _():
        out[...] = acc[...] if has_acc else jnp.zeros_like(out)

    n = out.shape[0]
    for w, klab, t in ((w0, klab0, t0), (w1, klab1, t1)):
        for i in range(n // TILE):
            keep = (klab[...] == occ[idx[8] * (n // TILE) + i]).astype(F32).astype(BF16)
            rows = pl.ds(i * TILE, TILE)
            masked[rows, :] = w[rows, :] * keep
        out[...] += jnp.dot(masked[...], t[0], preferred_element_type=F32)


def hole_part(idx, occ, klab, w, own, other, acc=None):
    n = own.shape[1]
    in_specs = [
        pl.BlockSpec((1, n), lambda j, idx, occ: (0, idx[j])),
        pl.BlockSpec((1, n), lambda j, idx, occ: (0, idx[4 + j])),
        pl.BlockSpec((n, n), lambda j, idx, occ: (0, idx[j])),
        pl.BlockSpec((n, n), lambda j, idx, occ: (0, idx[4 + j])),
        pl.BlockSpec((1, n, n), lambda j, idx, occ: (j, 0, 0)),
        pl.BlockSpec((1, n, n), lambda j, idx, occ: (j, 0, 0)),
    ]
    args = [klab, klab, w, w, own, other]
    if acc is not None:
        in_specs.append(pl.BlockSpec((n, n), lambda j, idx, occ: (0, 0)))
        args.append(acc)
    return pl.pallas_call(
        functools.partial(hole_kernel, has_acc=acc is not None),
        out_shape=jax.ShapeDtypeStruct((n, n), F32),
        grid_spec=pltpu.PrefetchScalarGridSpec(
            num_scalar_prefetch=2,
            grid=(NY,),
            in_specs=in_specs,
            out_specs=pl.BlockSpec((n, n), lambda j, idx, occ: (0, 0)),
            scratch_shapes=[pltpu.VMEM((n, n), BF16)],
        ),
        compiler_params=params(1),
        cost_estimate=cost(2 * NY, n),
        name="hole_part",
    )(idx, occ, *args)


def particle_kernel(idx, vir, qlab, ta, va, vb, acc, *rest, last):
    if last:
        oe, ve, res, masked, out = rest
    else:
        out, masked = rest
    j = pl.program_id(0)

    @pl.when(j == 0)
    def _():
        out[...] = acc[...]

    n = out.shape[0]
    block = idx[j]
    for v, base in ((va, 4), (vb, 8)):
        for i in range(NY):
            s = idx[base + i]
            keep = (qlab[...] == vir[block * (n // TILE) + s]).astype(F32).astype(BF16)
            masked[pl.ds(pl.multiple_of(s * TILE, TILE), TILE), :] = v[i, 0] * keep
    out[...] += jnp.dot(ta[0], masked[...], preferred_element_type=F32)
    if last:

        @pl.when(j == pl.num_programs(0) - 1)
        def _():
            res[...] = out[...].T / (ve[...] - oe[...])


def particle_part(idx, vir, qlab, ta, va, vb, acc, energies=None):
    n = acc.shape[0]
    last = energies is not None
    full = lambda *shape: pl.BlockSpec(shape, lambda j, idx, vir: (0,) * len(shape))
    in_specs = [
        full(1, n),
        pl.BlockSpec((1, n, n), lambda j, idx, vir: (j, 0, 0)),
        pl.BlockSpec((NY, 1, TILE, n), lambda j, idx, vir: (0, idx[j], 0, 0)),
        pl.BlockSpec((NY, 1, TILE, n), lambda j, idx, vir: (0, idx[j], 0, 0)),
        full(n, n),
    ]
    args = [qlab, ta, va, vb, acc]
    scratch = [pltpu.VMEM((n, n), BF16)]
    if last:
        in_specs += [full(1, n), full(n, 1)]
        args += list(energies)
        scratch.append(pltpu.VMEM((n, n), F32))
    return pl.pallas_call(
        functools.partial(particle_kernel, last=last),
        out_shape=jax.ShapeDtypeStruct((n, n), F32),
        grid_spec=pltpu.PrefetchScalarGridSpec(
            num_scalar_prefetch=2,
            grid=(ta.shape[0],),
            in_specs=in_specs,
            out_specs=full(n, n),
            scratch_shapes=scratch,
        ),
        compiler_params=params(1),
        cost_estimate=cost(ta.shape[0], n),
        name="particle_last" if last else "particle_part",
    )(idx, vir, *args)


def y_gather(a):
    half = a.shape[0] // 2
    up, down = shift(a, "y", NY, 1), shift(a, "y", NY, -1)
    far_a, far_b = shift(up[:half], "y", NY, 1), shift(down[half:], "y", NY, -1)
    return jnp.stack([a, up, down, jnp.concatenate([far_a, far_b])])


def per_device(t, w, v, occ, vir, occ_energy, vir_energy):
    n = t.shape[0]
    zh, y, c, zl, x = (lax.axis_index(a).astype(jnp.int32) for a in AXES)
    z = ("zh", "zl")
    tiles = n // TILE
    v_rows = lax.dynamic_slice_in_dim(v, (y * NC + c) * TILE, TILE)
    v_own = lax.all_to_all(v_rows, VIR, 1, 0, tiled=True).reshape(NZ * NX, TILE, n)

    ta0 = lax.all_gather(t, "x")
    l1, r1 = shift(t, z, 8, 1), shift(t, z, 8, -1)
    own_y = y_gather(t)
    ta1 = lax.all_gather(jnp.where(zl == 0, r1, l1), "x")
    l2, r2 = shift(l1, z, 8, 1), shift(r1, z, 8, -1)
    ta2 = lax.all_gather(jnp.where(zl == 0, r2, jnp.where(zl == 3, l2, r1)), "x")
    l3, r3 = shift(l2, z, 8, 1), shift(r2, z, 8, -1)
    ta3 = lax.all_gather(jnp.where(zl == 0, r3, jnp.where(zl == 1, r2, jnp.where(zl == 2, l2, l3))), "x")
    half = n // 2
    far = jnp.concatenate([shift(l3[:half], z, 8, 1), shift(r3[half:], z, 8, -1)])

    own_c = shift(own_y, "c", NC, 1)
    va = y_gather(v_own)
    vb = shift(va, "c", NC, 1)
    far_y = y_gather(far)
    far_c = shift(far_y, "c", NC, 1)

    rel = jnp.array([0, 3, 1, 2], jnp.int32)
    ys = (y + rel) % NY
    o = (zh * NY + y) * NC + c
    i_own = (zh * NY + ys) * NC
    i_far = ((1 - zh) * NY + ys) * NC
    klab = jnp.repeat(occ, TILE)[None, :]
    acc = hole_part(jnp.concatenate([i_own + c, i_own + 1 - c, o[None]]), occ, klab, w, own_y, own_c)

    qlab = jnp.repeat(lax.dynamic_slice_in_dim(vir, (zl * NX + x) * tiles, tiles), TILE)[None, :]
    s_own, s_other = ys * NC + c, ys * NC + 1 - c
    xs = jnp.arange(NX, dtype=jnp.int32)
    src = [zl, jnp.where(zl == 0, 1, zl - 1), jnp.where(zl == 0, 2, jnp.where(zl == 3, 1, zl + 1)), jnp.where(zl <= 1, 3, 0)]
    ids = [jnp.concatenate([s * NX + xs, s_own, s_other]) for s in src]
    acc = hole_part(jnp.concatenate([i_far + c, i_far + 1 - c, o[None]]), occ, klab, w, far_y, far_c, acc)
    acc = particle_part(ids[0], vir, qlab, ta0, va, vb, acc)
    acc = particle_part(ids[1], vir, qlab, ta1, va, vb, acc)
    acc = particle_part(ids[2], vir, qlab, ta2, va, vb, acc)
    return particle_part(ids[3], vir, qlab, ta3, va, vb, acc, (occ_energy[None, :], vir_energy[:, None]))


def solution(mesh):
    fine = Mesh(mesh.devices.reshape(2, NY, NC, NZ, NX), AXES)
    placed = (P(OCC, VIR), P(OCC, None), P(VIR, None), P(), P(), P(OCC), P(VIR))
    return jax.shard_map(
        per_device, mesh=fine, in_specs=placed, out_specs=P(VIR, OCC), check_vma=False
    )
```

```python
import functools

import jax
import jax.numpy as jnp
from jax import lax
from jax.experimental import pallas as pl
from jax.experimental.pallas import tpu as pltpu
from jax.sharding import Mesh, PartitionSpec as P

TILE = 64
F32, BF16 = jnp.float32, jnp.bfloat16
AXES = ("zh", "y", "c", "zl", "x")
OCC, VIR, YC = ("zh", "y", "c"), ("zl", "x"), ("y", "c")
NY, NC, NX, NZ = 4, 2, 4, 4
LIMIT = 60 * 1024 * 1024


def ring(n, d):
    return [(i, (i + d) % n) for i in range(n)]


def shift(a, axis, n, d):
    return lax.ppermute(a, axis, ring(n, d))


def params(n):
    return pltpu.CompilerParams(dimension_semantics=("arbitrary",) * n, vmem_limit_bytes=LIMIT)


def cost(blocks, n):
    return pl.CostEstimate(
        flops=2 * blocks * n**3, bytes_accessed=blocks * 2 * n * n * 2 + 4 * n * n, transcendentals=0
    )


def mask_of(labels, label):
    return (labels == label).astype(F32).astype(BF16)


def far_kernel(idx, occ, klab, w, t, acc, out, masked):
    j = pl.program_id(0)
    n = out.shape[0]
    for i in range(n // TILE):
        rows = pl.ds(i * TILE, TILE)
        masked[rows, :] = w[rows, :] * mask_of(klab[...], occ[idx[1] * (n // TILE) + i])
    part = jnp.dot(masked[...], t[...], preferred_element_type=F32)

    @pl.when(j == 0)
    def _():
        out[...] = acc[...] + part

    @pl.when(j > 0)
    def _():
        out[...] += part


def full(*shape):
    return pl.BlockSpec(shape, lambda *_: (0,) * len(shape))


def hole_kernel(idx, occ, klab, w, pair, g1, h1, g2, h2, *rest, has_acc):
    acc, (out, masked) = (rest[0], rest[1:]) if has_acc else (None, rest)
    j = pl.program_id(0)
    n = out.shape[0]
    core = idx[4]
    for i in range(n // TILE):
        rows = pl.ds(i * TILE, TILE)
        masked[rows, :] = w[rows, :] * mask_of(klab[...], occ[idx[5] * (n // TILE) + i])

    for step, t in enumerate((pair, g1, h1)):

        @pl.when(j == step)
        def _(step=step, t=t):
            part = jnp.dot(masked[...], t[...], preferred_element_type=F32)
            if step:
                out[...] += part
            elif has_acc:
                out[...] = acc[...] + part
            else:
                out[...] = part

    @pl.when(j == 3)
    def _():
        mine = masked[:, pl.ds(pl.multiple_of(core * n, n), n)]
        other = masked[:, pl.ds(pl.multiple_of((1 - core) * n, n), n)]
        out[...] += jnp.dot(mine, g2[...], preferred_element_type=F32) + jnp.dot(
            other, h2[...], preferred_element_type=F32
        )


def hole_part(idx, occ, klab, w, pair, g1, h1, g2, h2, acc=None):
    n = w.shape[0]
    in_specs = [
        pl.BlockSpec((1, 2 * n), lambda j, idx, occ: (0, idx[j])),
        pl.BlockSpec((n, 2 * n), lambda j, idx, occ: (0, idx[j])),
        full(2 * n, n),
        full(2 * n, n),
        full(2 * n, n),
        full(n, n),
        full(n, n),
    ]
    args = [klab, w, pair, g1, h1, g2, h2]
    if acc is not None:
        in_specs.append(full(n, n))
        args.append(acc)
    return pl.pallas_call(
        functools.partial(hole_kernel, has_acc=acc is not None),
        out_shape=jax.ShapeDtypeStruct((n, n), F32),
        grid_spec=pltpu.PrefetchScalarGridSpec(
            num_scalar_prefetch=2,
            grid=(NY,),
            in_specs=in_specs,
            out_specs=full(n, n),
            scratch_shapes=[pltpu.VMEM((n, 2 * n), BF16)],
        ),
        compiler_params=params(1),
        cost_estimate=cost(2 * NY, n),
        name="hole_part",
    )(idx, occ, *args)


def far_part(idx, occ, klab, w, t, acc):
    n = w.shape[0]
    steps = 2
    block = t.shape[0] // steps
    return pl.pallas_call(
        far_kernel,
        out_shape=jax.ShapeDtypeStruct((n, n), F32),
        grid_spec=pltpu.PrefetchScalarGridSpec(
            num_scalar_prefetch=2,
            grid=(steps,),
            in_specs=[
                pl.BlockSpec((1, block), lambda j, idx, occ: (0, idx[0] * steps + j)),
                pl.BlockSpec((n, block), lambda j, idx, occ: (0, idx[0] * steps + j)),
                pl.BlockSpec((block, n), lambda j, idx, occ: (j, 0)),
                full(n, n),
            ],
            out_specs=full(n, n),
            scratch_shapes=[pltpu.VMEM((n, block), BF16)],
        ),
        compiler_params=params(1),
        cost_estimate=cost(t.shape[0] // n, n),
        name="far_part",
    )(idx, occ, klab, w, t, acc)


def particle_kernel(idx, vir, qlab, *refs, count, split, last):
    nt = 2 if split else count
    tas, (pair, g1, h1, g2, h2, acc), rest = refs[:nt], refs[nt : nt + 6], refs[nt + 6 :]
    if last:
        oe, ve, out, masked, total = rest
    else:
        total, masked = rest
    j = pl.program_id(0)
    n = total.shape[0]
    tiles = n // TILE
    for k in range(count):
        label = lambda s: vir[(idx[j] * NX + idx[4 + k]) * tiles + s]
        b = 0 if count == 1 else idx[4 + k]
        for i, v in enumerate((pair, g1, h1)):
            s = idx[8 + i] * NC
            for e in range(NC):
                rows = pl.ds(pl.multiple_of(k * n + (s + e) * TILE, TILE), TILE)
                masked[rows, :] = v[e, b] * mask_of(qlab[...], label(s + e))
        for v, core in ((g2, idx[12]), (h2, 1 - idx[12])):
            s = idx[11] * NC + core
            rows = pl.ds(pl.multiple_of(k * n + s * TILE, TILE), TILE)
            masked[rows, :] = v[b] * mask_of(qlab[...], label(s))

    @pl.when(j == 0)
    def _():
        total[...] = acc[...]

    if split:
        for i, ta in enumerate(tas):
            rows = pl.ds(i * (n // 2), n // 2)
            total[rows, :] += jnp.dot(ta[0], masked[...], preferred_element_type=F32)
    else:
        blocks = jnp.concatenate([ta[0] for ta in tas], axis=1)
        total[...] += jnp.dot(blocks, masked[...], preferred_element_type=F32)

    if last:

        @pl.when(j == pl.num_programs(0) - 1)
        def _():
            out[...] = total[...].T / (ve[...] - oe[...])


def particle_part(idx, vir, qlab, tas, vs, acc, split=False, energies=None):
    n = acc.shape[0]
    last = energies is not None
    steps, count = tas[0].shape[0], 1 if split else len(tas)
    wide = pl.BlockSpec((NC, NX, TILE, n), lambda j, idx, vir: (0, idx[j], 0, 0))
    slim = pl.BlockSpec((NX, TILE, n), lambda j, idx, vir: (idx[j], 0, 0))
    if count == 1:
        wide = pl.BlockSpec((NC, 1, TILE, n), lambda j, idx, vir: (0, idx[j] * NX + idx[4], 0, 0))
        slim = pl.BlockSpec((1, TILE, n), lambda j, idx, vir: (idx[j] * NX + idx[4], 0, 0))
    at = pl.BlockSpec((1,) + tas[0].shape[1:], lambda j, *_: (j, 0, 0))
    in_specs = [full(1, n), *([at] * len(tas)), wide, wide, wide, slim, slim, full(n, n)]
    args = [qlab, *tas, *vs, acc]
    scratch = [pltpu.VMEM((count * n, n), BF16)]
    if last:
        in_specs += [full(1, n), full(n, 1)]
        args += list(energies)
        scratch.append(pltpu.VMEM((n, n), F32))
    return pl.pallas_call(
        functools.partial(particle_kernel, count=count, split=split, last=last),
        out_shape=jax.ShapeDtypeStruct((n, n), F32),
        grid_spec=pltpu.PrefetchScalarGridSpec(
            num_scalar_prefetch=2,
            grid=(steps,),
            in_specs=in_specs,
            out_specs=full(n, n),
            scratch_shapes=scratch,
        ),
        compiler_params=params(1),
        cost_estimate=cost(count * steps, n),
        name="particle_last" if last else "particle_part",
    )(idx, vir, *args)


def pick_kernel(idx, a, out):
    out[...] = a[...]


def pick(a, idx):
    block = (1,) + a.shape[1:]
    return pl.pallas_call(
        pick_kernel,
        out_shape=jax.ShapeDtypeStruct(idx.shape + a.shape[1:], a.dtype),
        grid_spec=pltpu.PrefetchScalarGridSpec(
            num_scalar_prefetch=1,
            grid=idx.shape,
            in_specs=[pl.BlockSpec(block, lambda j, idx: (idx[j], 0, 0))],
            out_specs=pl.BlockSpec(block, lambda j, idx: (j, 0, 0)),
        ),
        compiler_params=params(1),
        name="pick",
    )(idx, a)


AROUND = [(y * NC + c, (y + 1 - 2 * c) % NY * NC + c) for y in range(NY) for c in range(NC)]


def swap(a):
    return lax.ppermute(a, "c", ring(NC, 1))


def around(a):
    return lax.ppermute(a, YC, AROUND)


def tie(*arrays):
    return lax.optimization_barrier(arrays)


def per_device(t, w, v, occ, vir, occ_energy, vir_energy):
    n = t.shape[0]
    zh, y, c, zl, x = (lax.axis_index(a).astype(jnp.int32) for a in AXES)
    z = ("zh", "zl")
    tiles, half = n // TILE, n // 2
    both = lambda a, b: jnp.where(c == 0, jnp.stack([a, b]), jnp.stack([b, a]))
    mine = lambda a: jnp.where(c == 0, a[0], a[1])

    zag = lax.all_gather(t, z)
    v_rows = lax.dynamic_slice_in_dim(v, (y * NC + c) * TILE, TILE)
    v_own = lax.all_to_all(v_rows, VIR, 1, 0, tiled=True).reshape(NZ * NX, TILE, n)
    x1, x3 = shift(t, "x", NX, 1), shift(t, "x", NX, -1)
    pair = both(t, swap(t))
    g1 = around(pair)
    x1, x3, g1 = tie(x1, x3, g1)
    x2a, x2b = shift(x1[:half], "x", NX, 1), shift(x3[half:], "x", NX, -1)
    g2, h1 = around(mine(g1)), swap(g1)
    x2a, x2b, g2, h1, v_own = tie(x2a, x2b, g2, h1, v_own)

    o = (zh * NY + y) * NC + c
    klab = jnp.repeat(occ, TILE)[None, :]
    flat = lambda a: a.reshape(-1, n)
    near = y + 2 * c - 1
    ys = jnp.stack([y, near, 2 * y - near, y + 2]) % NY
    xs = (x + jnp.array([0, 3, 1, 2], jnp.int32)) % NX

    v_pair = both(v_own, swap(v_own))
    vg1 = around(v_pair)
    x2 = jnp.concatenate([x2a, x2b])
    h2 = swap(g2)
    i_own = jnp.concatenate([zh * NY + ys, c[None], o[None]])
    acc = hole_part(i_own, occ, klab, w, flat(pair), flat(g1), flat(h1), g2, h2)
    others = pick(zag, zh * NZ + (zl + 1 + jnp.arange(NZ - 1, dtype=jnp.int32)) % NZ)
    far = pick(zag, ((1 - zh) * NZ + zl)[None]).reshape(n, n)
    others, far, vg1, acc = tie(others, far, vg1, acc)

    far_t = lax.all_gather(far, YC, tiled=True)
    o1, o3 = shift(others, "x", NX, 1), shift(others, "x", NX, -1)
    vg2, vh1 = around(mine(vg1)), swap(vg1)
    vh2 = swap(vg2)
    qlab = jnp.repeat(lax.dynamic_slice_in_dim(vir, (zl * NX + x) * tiles, tiles), TILE)[None, :]
    ids = lambda d, at: jnp.concatenate([(zl + d + jnp.arange(NZ, dtype=jnp.int32)) % NZ, at, ys, c[None]])
    vs = (v_pair, vg1, vh1, vg2, vh2)
    acc = particle_part(ids(0, xs), vir, qlab, (t[None], x1[None], x3[None], x2[None]), vs, acc)
    o1, o3, acc = tie(o1, o3, acc)

    o2 = (shift(o1[:, :half], "x", NX, 1), shift(o3[:, half:], "x", NX, -1))
    acc = particle_part(ids(1, xs), vir, qlab, (others, o1, o3), vs, acc)
    acc = far_part(jnp.stack([1 - zh, o]), occ, klab, w, far_t, acc)
    energies = (occ_energy[None, :], vir_energy[:, None])
    return particle_part(ids(1, xs[::-1]), vir, qlab, o2, vs, acc, True, energies)


def solution(mesh):
    fine = Mesh(mesh.devices.reshape(2, NY, NC, NZ, NX), AXES)
    placed = (P(OCC, VIR), P(OCC, None), P(VIR, None), P(), P(), P(OCC), P(VIR))
    return jax.shard_map(
        per_device, mesh=fine, in_specs=placed, out_specs=P(VIR, OCC), check_vma=False
    )
```

```python
import functools

import jax
import jax.numpy as jnp
from jax import lax
from jax.experimental import pallas as pl
from jax.experimental.pallas import tpu as pltpu
from jax.sharding import Mesh, PartitionSpec as P

TILE = 64
F32, BF16 = jnp.float32, jnp.bfloat16
AXES = ("zh", "y", "c", "zl", "x")
OCC, VIR, YC = ("zh", "y", "c"), ("zl", "x"), ("y", "c")
NY, NC, NX, NZ = 4, 2, 4, 4
LIMIT = 60 * 1024 * 1024


def ring(n, d):
    return [(i, (i + d) % n) for i in range(n)]


def shift(a, axis, n, d):
    return lax.ppermute(a, axis, ring(n, d))


def params(n):
    return pltpu.CompilerParams(dimension_semantics=("arbitrary",) * n, vmem_limit_bytes=LIMIT)


def cost(blocks, n):
    return pl.CostEstimate(
        flops=2 * blocks * n**3, bytes_accessed=blocks * 2 * n * n * 2 + 4 * n * n, transcendentals=0
    )


def mask_of(labels, label):
    return (labels == label).astype(F32).astype(BF16)


def far_kernel(idx, occ, klab, w, t, acc, out, masked):
    j = pl.program_id(0)
    n = out.shape[0]
    for i in range(n // TILE):
        rows = pl.ds(i * TILE, TILE)
        masked[rows, :] = w[rows, :] * mask_of(klab[...], occ[idx[1] * (n // TILE) + i])
    part = jnp.dot(masked[...], t[...], preferred_element_type=F32)

    @pl.when(j == 0)
    def _():
        out[...] = acc[...] + part

    @pl.when(j > 0)
    def _():
        out[...] += part


def full(*shape):
    return pl.BlockSpec(shape, lambda *_: (0,) * len(shape))


def hole_kernel(idx, occ, klab, w, pair, g1, h1, g2, h2, *rest, has_acc):
    acc, (out, masked) = (rest[0], rest[1:]) if has_acc else (None, rest)
    j = pl.program_id(0)
    n = out.shape[0]
    core = idx[4]
    for i in range(n // TILE):
        rows = pl.ds(i * TILE, TILE)
        masked[rows, :] = w[rows, :] * mask_of(klab[...], occ[idx[5] * (n // TILE) + i])

    for step, t in enumerate((pair, g1, h1)):

        @pl.when(j == step)
        def _(step=step, t=t):
            part = jnp.dot(masked[...], t[...], preferred_element_type=F32)
            if step:
                out[...] += part
            elif has_acc:
                out[...] = acc[...] + part
            else:
                out[...] = part

    @pl.when(j == 3)
    def _():
        mine = masked[:, pl.ds(pl.multiple_of(core * n, n), n)]
        other = masked[:, pl.ds(pl.multiple_of((1 - core) * n, n), n)]
        out[...] += jnp.dot(mine, g2[...], preferred_element_type=F32) + jnp.dot(
            other, h2[...], preferred_element_type=F32
        )


def hole_part(idx, occ, klab, w, pair, g1, h1, g2, h2, acc=None):
    n = w.shape[0]
    in_specs = [
        pl.BlockSpec((1, 2 * n), lambda j, idx, occ: (0, idx[j])),
        pl.BlockSpec((n, 2 * n), lambda j, idx, occ: (0, idx[j])),
        full(2 * n, n),
        full(2 * n, n),
        full(2 * n, n),
        full(n, n),
        full(n, n),
    ]
    args = [klab, w, pair, g1, h1, g2, h2]
    if acc is not None:
        in_specs.append(full(n, n))
        args.append(acc)
    return pl.pallas_call(
        functools.partial(hole_kernel, has_acc=acc is not None),
        out_shape=jax.ShapeDtypeStruct((n, n), F32),
        grid_spec=pltpu.PrefetchScalarGridSpec(
            num_scalar_prefetch=2,
            grid=(NY,),
            in_specs=in_specs,
            out_specs=full(n, n),
            scratch_shapes=[pltpu.VMEM((n, 2 * n), BF16)],
        ),
        compiler_params=params(1),
        cost_estimate=cost(2 * NY, n),
        name="hole_part",
    )(idx, occ, *args)


def far_part(idx, occ, klab, w, t, acc):
    n = w.shape[0]
    steps = 2
    block = t.shape[0] // steps
    return pl.pallas_call(
        far_kernel,
        out_shape=jax.ShapeDtypeStruct((n, n), F32),
        grid_spec=pltpu.PrefetchScalarGridSpec(
            num_scalar_prefetch=2,
            grid=(steps,),
            in_specs=[
                pl.BlockSpec((1, block), lambda j, idx, occ: (0, idx[0] * steps + j)),
                pl.BlockSpec((n, block), lambda j, idx, occ: (0, idx[0] * steps + j)),
                pl.BlockSpec((block, n), lambda j, idx, occ: (j, 0)),
                full(n, n),
            ],
            out_specs=full(n, n),
            scratch_shapes=[pltpu.VMEM((n, block), BF16)],
        ),
        compiler_params=params(1),
        cost_estimate=cost(t.shape[0] // n, n),
        name="far_part",
    )(idx, occ, klab, w, t, acc)


def particle_kernel(idx, vir, qlab, *refs, count, split, last):
    nt = 2 if split else count
    tas, (pair, g1, h1, g2, h2, acc), rest = refs[:nt], refs[nt : nt + 6], refs[nt + 6 :]
    if last:
        oe, ve, out, masked, total = rest
    else:
        total, masked = rest
    j = pl.program_id(0)
    n = total.shape[0]
    tiles = n // TILE
    for k in range(count):
        label = lambda s: vir[(idx[j] * NX + idx[4 + k]) * tiles + s]
        b = 0 if count == 1 else idx[4 + k]
        for i, v in enumerate((pair, g1, h1)):
            s = idx[8 + i] * NC
            for e in range(NC):
                rows = pl.ds(pl.multiple_of(k * n + (s + e) * TILE, TILE), TILE)
                masked[rows, :] = v[e, b] * mask_of(qlab[...], label(s + e))
        for v, core in ((g2, idx[12]), (h2, 1 - idx[12])):
            s = idx[11] * NC + core
            rows = pl.ds(pl.multiple_of(k * n + s * TILE, TILE), TILE)
            masked[rows, :] = v[b] * mask_of(qlab[...], label(s))

    @pl.when(j == 0)
    def _():
        total[...] = acc[...]

    if split:
        for i, ta in enumerate(tas):
            rows = pl.ds(i * (n // 2), n // 2)
            total[rows, :] += jnp.dot(ta[0], masked[...], preferred_element_type=F32)
    else:
        blocks = jnp.concatenate([ta[0] for ta in tas], axis=1)
        total[...] += jnp.dot(blocks, masked[...], preferred_element_type=F32)

    if last:

        @pl.when(j == pl.num_programs(0) - 1)
        def _():
            out[...] = total[...].T / (ve[...] - oe[...])


def particle_part(idx, vir, qlab, tas, vs, acc, split=False, energies=None):
    n = acc.shape[0]
    last = energies is not None
    steps, count = tas[0].shape[0], 1 if split else len(tas)
    wide = pl.BlockSpec((NC, NX, TILE, n), lambda j, idx, vir: (0, idx[j], 0, 0))
    slim = pl.BlockSpec((NX, TILE, n), lambda j, idx, vir: (idx[j], 0, 0))
    if count == 1:
        wide = pl.BlockSpec((NC, 1, TILE, n), lambda j, idx, vir: (0, idx[j] * NX + idx[4], 0, 0))
        slim = pl.BlockSpec((1, TILE, n), lambda j, idx, vir: (idx[j] * NX + idx[4], 0, 0))
    at = pl.BlockSpec((1,) + tas[0].shape[1:], lambda j, *_: (j, 0, 0))
    in_specs = [full(1, n), *([at] * len(tas)), wide, wide, wide, slim, slim, full(n, n)]
    args = [qlab, *tas, *vs, acc]
    scratch = [pltpu.VMEM((count * n, n), BF16)]
    if last:
        in_specs += [full(1, n), full(n, 1)]
        args += list(energies)
        scratch.append(pltpu.VMEM((n, n), F32))
    return pl.pallas_call(
        functools.partial(particle_kernel, count=count, split=split, last=last),
        out_shape=jax.ShapeDtypeStruct((n, n), F32),
        grid_spec=pltpu.PrefetchScalarGridSpec(
            num_scalar_prefetch=2,
            grid=(steps,),
            in_specs=in_specs,
            out_specs=full(n, n),
            scratch_shapes=scratch,
        ),
        compiler_params=params(1),
        cost_estimate=cost(count * steps, n),
        name="particle_last" if last else "particle_part",
    )(idx, vir, *args)


def pick_kernel(idx, a, out):
    out[...] = a[...]


def pick(a, idx):
    block = (1,) + a.shape[1:]
    return pl.pallas_call(
        pick_kernel,
        out_shape=jax.ShapeDtypeStruct(idx.shape + a.shape[1:], a.dtype),
        grid_spec=pltpu.PrefetchScalarGridSpec(
            num_scalar_prefetch=1,
            grid=idx.shape,
            in_specs=[pl.BlockSpec(block, lambda j, idx: (idx[j], 0, 0))],
            out_specs=pl.BlockSpec(block, lambda j, idx: (j, 0, 0)),
        ),
        compiler_params=params(1),
        name="pick",
    )(idx, a)


AROUND = [(y * NC + c, (y + 1 - 2 * c) % NY * NC + c) for y in range(NY) for c in range(NC)]


def swap(a):
    return lax.ppermute(a, "c", ring(NC, 1))


def around(a):
    return lax.ppermute(a, YC, AROUND)


def tie(*arrays):
    return lax.optimization_barrier(arrays)


def per_device(t, w, v, occ, vir, occ_energy, vir_energy):
    n = t.shape[0]
    zh, y, c, zl, x = (lax.axis_index(a).astype(jnp.int32) for a in AXES)
    z = ("zh", "zl")
    tiles, half = n // TILE, n // 2
    both = lambda a, b: jnp.where(c == 0, jnp.stack([a, b]), jnp.stack([b, a]))
    mine = lambda a: jnp.where(c == 0, a[0], a[1])

    zag = lax.all_gather(t, z)
    v_rows = lax.dynamic_slice_in_dim(v, (y * NC + c) * TILE, TILE)
    v_rows = jnp.swapaxes(v_rows.reshape(TILE, NZ * NX, n), 0, 1)
    v_rows, t0 = tie(v_rows, t)
    v_own = lax.all_to_all(v_rows, VIR, 0, 0, tiled=True)
    x1, x3 = shift(t0, "x", NX, 1), shift(t0, "x", NX, -1)
    pair = both(t0, swap(t0))
    g1 = around(pair)
    x1, x3, g1 = tie(x1, x3, g1)
    x2a, x2b = shift(x1[:half], "x", NX, 1), shift(x3[half:], "x", NX, -1)
    g2, h1 = around(mine(g1)), swap(g1)
    x2a, x2b, g2, h1, v_own = tie(x2a, x2b, g2, h1, v_own)

    o = (zh * NY + y) * NC + c
    klab = jnp.repeat(occ, TILE)[None, :]
    flat = lambda a: a.reshape(-1, n)
    near = y + 2 * c - 1
    ys = jnp.stack([y, near, 2 * y - near, y + 2]) % NY
    xs = (x + jnp.array([0, 3, 1, 2], jnp.int32)) % NX

    v_pair = both(v_own, swap(v_own))
    vg1 = around(v_pair)
    x2 = jnp.concatenate([x2a, x2b])
    h2 = swap(g2)
    i_own = jnp.concatenate([zh * NY + ys, c[None], o[None]])
    acc = hole_part(i_own, occ, klab, w, flat(pair), flat(g1), flat(h1), g2, h2)
    others = pick(zag, zh * NZ + (zl + 1 + jnp.arange(NZ - 1, dtype=jnp.int32)) % NZ)
    far = pick(zag, ((1 - zh) * NZ + zl)[None]).reshape(n, n)
    others, far, vg1, acc = tie(others, far, vg1, acc)

    far_t = lax.all_gather(far, YC, tiled=True)
    o1, o3 = shift(others, "x", NX, 1), shift(others, "x", NX, -1)
    vg2, vh1 = around(mine(vg1)), swap(vg1)
    vh2 = swap(vg2)
    qlab = jnp.repeat(lax.dynamic_slice_in_dim(vir, (zl * NX + x) * tiles, tiles), TILE)[None, :]
    ids = lambda d, at: jnp.concatenate([(zl + d + jnp.arange(NZ, dtype=jnp.int32)) % NZ, at, ys, c[None]])
    vs = (v_pair, vg1, vh1, vg2, vh2)
    acc = particle_part(ids(0, xs), vir, qlab, (t[None], x1[None], x3[None], x2[None]), vs, acc)
    o1, o3, acc = tie(o1, o3, acc)

    o2 = (shift(o1[:, :half], "x", NX, 1), shift(o3[:, half:], "x", NX, -1))
    acc = particle_part(ids(1, xs), vir, qlab, (others, o1, o3), vs, acc)
    acc = far_part(jnp.stack([1 - zh, o]), occ, klab, w, far_t, acc)
    energies = (occ_energy[None, :], vir_energy[:, None])
    return particle_part(ids(1, xs[::-1]), vir, qlab, o2, vs, acc, True, energies)


def solution(mesh):
    fine = Mesh(mesh.devices.reshape(2, NY, NC, NZ, NX), AXES)
    placed = (P(OCC, VIR), P(OCC, None), P(VIR, None), P(), P(), P(OCC), P(VIR))
    return jax.shard_map(
        per_device, mesh=fine, in_specs=placed, out_specs=P(VIR, OCC), check_vma=False
    )
```

```python
import functools

import jax
import jax.numpy as jnp
from jax import lax
from jax.experimental import pallas as pl
from jax.experimental.pallas import tpu as pltpu
from jax.sharding import Mesh, PartitionSpec as P

TILE = 64
F32, BF16 = jnp.float32, jnp.bfloat16
AXES = ("zh", "y", "c", "zl", "x")
OCC, VIR, YC = ("zh", "y", "c"), ("zl", "x"), ("y", "c")
NY, NC, NX, NZ = 4, 2, 4, 4
LIMIT = 60 * 1024 * 1024


def ring(n, d):
    return [(i, (i + d) % n) for i in range(n)]


def shift(a, axis, n, d):
    return lax.ppermute(a, axis, ring(n, d))


def params(n):
    return pltpu.CompilerParams(dimension_semantics=("arbitrary",) * n, vmem_limit_bytes=LIMIT)


def cost(blocks, n):
    return pl.CostEstimate(
        flops=2 * blocks * n**3, bytes_accessed=blocks * 2 * n * n * 2 + 4 * n * n, transcendentals=0
    )


def mask_of(labels, label):
    return (labels == label).astype(F32).astype(BF16)


def far_kernel(idx, occ, klab, w, t, acc, out, masked):
    j = pl.program_id(0)
    n = out.shape[0]
    for i in range(n // TILE):
        rows = pl.ds(i * TILE, TILE)
        masked[rows, :] = w[rows, :] * mask_of(klab[...], occ[idx[1] * (n // TILE) + i])
    part = jnp.dot(masked[...], t[...], preferred_element_type=F32)

    @pl.when(j == 0)
    def _():
        out[...] = acc[...] + part

    @pl.when(j > 0)
    def _():
        out[...] += part


def full(*shape):
    return pl.BlockSpec(shape, lambda *_: (0,) * len(shape))


def hole_kernel(idx, occ, klab, w, pair, g1, h1, g2, h2, *rest, has_acc):
    acc, (out, masked) = (rest[0], rest[1:]) if has_acc else (None, rest)
    j = pl.program_id(0)
    n = out.shape[0]
    core = idx[4]
    for i in range(n // TILE):
        rows = pl.ds(i * TILE, TILE)
        masked[rows, :] = w[rows, :] * mask_of(klab[...], occ[idx[5] * (n // TILE) + i])

    for step, t in enumerate((pair, g1, h1)):

        @pl.when(j == step)
        def _(step=step, t=t):
            part = jnp.dot(masked[...], t[...], preferred_element_type=F32)
            if step:
                out[...] += part
            elif has_acc:
                out[...] = acc[...] + part
            else:
                out[...] = part

    @pl.when(j == 3)
    def _():
        mine = masked[:, pl.ds(pl.multiple_of(core * n, n), n)]
        other = masked[:, pl.ds(pl.multiple_of((1 - core) * n, n), n)]
        out[...] += jnp.dot(mine, g2[...], preferred_element_type=F32) + jnp.dot(
            other, h2[...], preferred_element_type=F32
        )


def hole_part(idx, occ, klab, w, pair, g1, h1, g2, h2, acc=None):
    n = w.shape[0]
    in_specs = [
        pl.BlockSpec((1, 2 * n), lambda j, idx, occ: (0, idx[j])),
        pl.BlockSpec((n, 2 * n), lambda j, idx, occ: (0, idx[j])),
        full(2 * n, n),
        full(2 * n, n),
        full(2 * n, n),
        full(n, n),
        full(n, n),
    ]
    args = [klab, w, pair, g1, h1, g2, h2]
    if acc is not None:
        in_specs.append(full(n, n))
        args.append(acc)
    return pl.pallas_call(
        functools.partial(hole_kernel, has_acc=acc is not None),
        out_shape=jax.ShapeDtypeStruct((n, n), F32),
        grid_spec=pltpu.PrefetchScalarGridSpec(
            num_scalar_prefetch=2,
            grid=(NY,),
            in_specs=in_specs,
            out_specs=full(n, n),
            scratch_shapes=[pltpu.VMEM((n, 2 * n), BF16)],
        ),
        compiler_params=params(1),
        cost_estimate=cost(2 * NY, n),
        name="hole_part",
    )(idx, occ, *args)


def far_part(idx, occ, klab, w, t, acc):
    n = w.shape[0]
    steps = 2
    block = t.shape[0] // steps
    return pl.pallas_call(
        far_kernel,
        out_shape=jax.ShapeDtypeStruct((n, n), F32),
        grid_spec=pltpu.PrefetchScalarGridSpec(
            num_scalar_prefetch=2,
            grid=(steps,),
            in_specs=[
                pl.BlockSpec((1, block), lambda j, idx, occ: (0, idx[0] * steps + j)),
                pl.BlockSpec((n, block), lambda j, idx, occ: (0, idx[0] * steps + j)),
                pl.BlockSpec((block, n), lambda j, idx, occ: (j, 0)),
                full(n, n),
            ],
            out_specs=full(n, n),
            scratch_shapes=[pltpu.VMEM((n, block), BF16)],
        ),
        compiler_params=params(1),
        cost_estimate=cost(t.shape[0] // n, n),
        name="far_part",
    )(idx, occ, klab, w, t, acc)


def particle_kernel(idx, vir, qlab, *refs, count, split, last):
    nt = 2 if split else count
    tas, (pair, g1, h1, g2, h2, acc), rest = refs[:nt], refs[nt : nt + 6], refs[nt + 6 :]
    if last:
        oe, ve, out, masked, total = rest
    else:
        total, masked = rest
    j = pl.program_id(0)
    n = total.shape[0]
    tiles = n // TILE
    for k in range(count):
        label = lambda s: vir[(idx[j] * NX + idx[4 + k]) * tiles + s]
        b = 0 if count == 1 else idx[4 + k]
        for i, v in enumerate((pair, g1, h1)):
            s = idx[8 + i] * NC
            for e in range(NC):
                rows = pl.ds(pl.multiple_of(k * n + (s + e) * TILE, TILE), TILE)
                masked[rows, :] = v[e, b] * mask_of(qlab[...], label(s + e))
        for v, core in ((g2, idx[12]), (h2, 1 - idx[12])):
            s = idx[11] * NC + core
            rows = pl.ds(pl.multiple_of(k * n + s * TILE, TILE), TILE)
            masked[rows, :] = v[b] * mask_of(qlab[...], label(s))

    if split:
        parts = [jnp.dot(ta[0], masked[...], preferred_element_type=F32) for ta in tas]
        part = jnp.concatenate(parts, axis=0)
    else:
        blocks = jnp.concatenate([ta[0] for ta in tas], axis=1)
        part = jnp.dot(blocks, masked[...], preferred_element_type=F32)

    @pl.when(j == 0)
    def _():
        total[...] = acc[...] + part

    @pl.when(j > 0)
    def _():
        total[...] += part

    if last:

        @pl.when(j == pl.num_programs(0) - 1)
        def _():
            out[...] = total[...].T / (ve[...] - oe[...])


def particle_part(idx, vir, qlab, tas, vs, acc, split=False, energies=None):
    n = acc.shape[0]
    last = energies is not None
    steps, count = tas[0].shape[0], 1 if split else len(tas)
    wide = pl.BlockSpec((NC, NX, TILE, n), lambda j, idx, vir: (0, idx[j], 0, 0))
    slim = pl.BlockSpec((NX, TILE, n), lambda j, idx, vir: (idx[j], 0, 0))
    if count == 1:
        wide = pl.BlockSpec((NC, 1, TILE, n), lambda j, idx, vir: (0, idx[j] * NX + idx[4], 0, 0))
        slim = pl.BlockSpec((1, TILE, n), lambda j, idx, vir: (idx[j] * NX + idx[4], 0, 0))
    at = pl.BlockSpec((1,) + tas[0].shape[1:], lambda j, *_: (j, 0, 0))
    in_specs = [full(1, n), *([at] * len(tas)), wide, wide, wide, slim, slim, full(n, n)]
    args = [qlab, *tas, *vs, acc]
    scratch = [pltpu.VMEM((count * n, n), BF16)]
    if last:
        in_specs += [full(1, n), full(n, 1)]
        args += list(energies)
        scratch.append(pltpu.VMEM((n, n), F32))
    return pl.pallas_call(
        functools.partial(particle_kernel, count=count, split=split, last=last),
        out_shape=jax.ShapeDtypeStruct((n, n), F32),
        grid_spec=pltpu.PrefetchScalarGridSpec(
            num_scalar_prefetch=2,
            grid=(steps,),
            in_specs=in_specs,
            out_specs=full(n, n),
            scratch_shapes=scratch,
        ),
        compiler_params=params(1),
        cost_estimate=cost(count * steps, n),
        name="particle_last" if last else "particle_part",
    )(idx, vir, *args)


def pick_kernel(idx, a, out):
    out[...] = a[...]


def pick(a, idx):
    block = (1,) + a.shape[1:]
    return pl.pallas_call(
        pick_kernel,
        out_shape=jax.ShapeDtypeStruct(idx.shape + a.shape[1:], a.dtype),
        grid_spec=pltpu.PrefetchScalarGridSpec(
            num_scalar_prefetch=1,
            grid=idx.shape,
            in_specs=[pl.BlockSpec(block, lambda j, idx: (idx[j], 0, 0))],
            out_specs=pl.BlockSpec(block, lambda j, idx: (j, 0, 0)),
        ),
        compiler_params=params(1),
        name="pick",
    )(idx, a)


AROUND = [(y * NC + c, (y + 1 - 2 * c) % NY * NC + c) for y in range(NY) for c in range(NC)]


def swap(a):
    return lax.ppermute(a, "c", ring(NC, 1))


def around(a):
    return lax.ppermute(a, YC, AROUND)


def tie(*arrays):
    return lax.optimization_barrier(arrays)


def per_device(t, w, v, occ, vir, occ_energy, vir_energy):
    n = t.shape[0]
    zh, y, c, zl, x = (lax.axis_index(a).astype(jnp.int32) for a in AXES)
    z = ("zh", "zl")
    tiles, half = n // TILE, n // 2
    both = lambda a, b: jnp.where(c == 0, jnp.stack([a, b]), jnp.stack([b, a]))
    mine = lambda a: jnp.where(c == 0, a[0], a[1])

    zag = lax.all_gather(t, z)
    v_rows = lax.dynamic_slice_in_dim(v, (y * NC + c) * TILE, TILE)
    v_rows = jnp.swapaxes(v_rows.reshape(TILE, NZ * NX, n), 0, 1)
    v_rows, t0 = tie(v_rows, t)
    v_own = lax.all_to_all(v_rows, VIR, 0, 0, tiled=True)
    x1, x3 = shift(t0, "x", NX, 1), shift(t0, "x", NX, -1)
    pair = both(t0, swap(t0))
    g1 = around(pair)
    x1, x3, g1 = tie(x1, x3, g1)
    x2a, x2b = shift(x1[:half], "x", NX, 1), shift(x3[half:], "x", NX, -1)
    g2, h1 = around(mine(g1)), swap(g1)
    x2a, x2b, g2, h1, v_own = tie(x2a, x2b, g2, h1, v_own)

    o = (zh * NY + y) * NC + c
    klab = jnp.repeat(occ, TILE)[None, :]
    flat = lambda a: a.reshape(-1, n)
    near = y + 2 * c - 1
    ys = jnp.stack([y, near, 2 * y - near, y + 2]) % NY
    xs = (x + jnp.array([0, 3, 1, 2], jnp.int32)) % NX

    v_pair = both(v_own, swap(v_own))
    vg1 = around(v_pair)
    x2 = jnp.concatenate([x2a, x2b])
    h2 = swap(g2)
    i_own = jnp.concatenate([zh * NY + ys, c[None], o[None]])
    acc = hole_part(i_own, occ, klab, w, flat(pair), flat(g1), flat(h1), g2, h2)
    others = pick(zag, zh * NZ + (zl + 1 + jnp.arange(NZ - 1, dtype=jnp.int32)) % NZ)
    far = pick(zag, ((1 - zh) * NZ + zl)[None]).reshape(n, n)
    others, far, vg1, acc = tie(others, far, vg1, acc)

    far_t = lax.all_gather(far, YC, tiled=True)
    o1, o3 = shift(others, "x", NX, 1), shift(others, "x", NX, -1)
    vg2, vh1 = around(mine(vg1)), swap(vg1)
    vh2 = swap(vg2)
    qlab = jnp.repeat(lax.dynamic_slice_in_dim(vir, (zl * NX + x) * tiles, tiles), TILE)[None, :]
    ids = lambda d, at: jnp.concatenate([(zl + d + jnp.arange(NZ, dtype=jnp.int32)) % NZ, at, ys, c[None]])
    vs = (v_pair, vg1, vh1, vg2, vh2)
    acc = particle_part(ids(0, xs), vir, qlab, (t[None], x1[None], x3[None], x2[None]), vs, acc)
    o1, o3, acc = tie(o1, o3, acc)

    o2 = (shift(o1[:, :half], "x", NX, 1), shift(o3[:, half:], "x", NX, -1))
    acc = particle_part(ids(1, xs), vir, qlab, (others, o1, o3), vs, acc)
    acc = far_part(jnp.stack([1 - zh, o]), occ, klab, w, far_t, acc)
    energies = (occ_energy[None, :], vir_energy[:, None])
    return particle_part(ids(1, xs[::-1]), vir, qlab, o2, vs, acc, True, energies)


def solution(mesh):
    fine = Mesh(mesh.devices.reshape(2, NY, NC, NZ, NX), AXES)
    placed = (P(OCC, VIR), P(OCC, None), P(VIR, None), P(), P(), P(OCC), P(VIR))
    return jax.shard_map(
        per_device, mesh=fine, in_specs=placed, out_specs=P(VIR, OCC), check_vma=False
    )
```
